768 devices in a mesh: ctx: 96 (over z, y), fsdp: 8 (over x, core).
Axes of the slice: x: 4, y: 8, z: 12, core: 2. Of those that a mesh axis runs over, the one named last changes fastest.
Arguments:
- values: bfloat16 [8, 12288, 4096], P('fsdp', 'ctx'), may hold values from -6 to 6
- cotangent: bfloat16 [8, 12288, 4096], P('fsdp', 'ctx'), may hold values from -6 to 6
- seg_ids: int32 [8, 12288], P('fsdp', 'ctx'), may hold values from 0 to 3, never falling along the last dimension, each value on 1 to 6144 neighbouring positions
- filters: bfloat16 [256, 128], P('fsdp'), may hold values from -0.5 to 0.5
- skip_gain: bfloat16 [4096], P('fsdp'), may hold values from -4 to 4
Outputs:
- mixed: bfloat16 [8, 12288, 4096], P('fsdp', 'ctx')
- grad_values: bfloat16 [8, 12288, 4096], P('fsdp', 'ctx')
- grad_filters: float32 [256, 128], P('fsdp')
- grad_skip: float32 [4096], P('fsdp')
The draws below stay inside these ranges and needn't reach their ends.
Inputs may be any that keep to these rules, and one draw needn't show every extreme that they name: `seg_ids`: along each stream document numbers start at 0 and never fall; each document covers 1 to 6144 positions, and one covers exactly that many.
All inputs are finite; a program needn't handle non-finite values.
Results may differ from the reference program's by a relative error of at most 0.001.
Values may be sent and summed in bfloat16 or wider, within the bound.
A program may use at most 64 MiB of HBM per device.

```python
import math
import jax
import jax.numpy as jnp
import numpy as np
from jax import lax

CH = 4096
GSIZE = 16
TAPS = 128
TOK_DEV = 128
GROUPS = 256
STREAMS = 8
SEQ = 12288


def with_spikes(result, own_key, source, target, parts, factor):
    def block_of(dim):
        return (jnp.arange(result.shape[dim]) // (result.shape[dim] // parts)).reshape((-1,) + (1,) * (result.ndim - 1 - dim))

    near = jax.random.permutation(own_key, parts)[block_of(target)]
    far = (block_of(target) + parts // 2) % parts
    return jnp.where((block_of(source) == near) | (block_of(source) == far), factor * result, result)


def steps_of(own_key, dims, pieces, least, top_value):
    def one(position, blocks):
        heights = jax.random.uniform(jax.random.fold_in(jax.random.fold_in(own_key, 6), position), (blocks,), jnp.float32, least / len(pieces), top_value / len(pieces))
        return jnp.repeat(jnp.exp(heights), dims[position] // blocks).reshape((-1,) + (1,) * (len(dims) - position - 1))

    factor_of = one(*pieces[0])
    for cut in pieces[1:]:
        factor_of = factor_of * one(*cut)
    return factor_of


def split_up(amount, total, bound, slope):
    portions = [(1 << 20) // math.isqrt(rank ** slope) + 1 for rank in range(2, amount + 1)]
    surplus, given = total - bound - (amount - 1), [1] * (amount - 1)
    while surplus > 0:
        free = [i for i in range(amount - 1) if given[i] < bound]
        whole, budget = sum([portions[i] for i in free]), surplus
        for i in free:
            extra = min(bound - given[i], max(1, budget * portions[i] // whole), surplus)
            given[i] = given[i] + extra
            surplus = surplus - extra
    return np.array([bound] + given)


def uneven(rng, number_of, total, bound, slope):
    if number_of == 2:
        one = jax.random.randint(rng, (), max(1, total - bound), min(bound, total - 1) + 1)
        return jnp.stack([one, total - one])
    lengths = jnp.asarray(split_up(number_of, total, bound, slope), jnp.int32)
    pairs = (number_of - 1) // 2
    giver, receiver = lengths[1:1 + 2 * pairs:2], lengths[2:2 + 2 * pairs:2]
    slack = jnp.minimum(giver - 1, bound - receiver)
    passed = jax.random.randint(jax.random.fold_in(rng, 1), (pairs,), 0, 1 << 20) % (slack + 1)
    lengths = lengths.at[1:1 + 2 * pairs:2].set(giver - passed).at[2:2 + 2 * pairs:2].set(receiver + passed)
    return lengths[jax.random.permutation(jax.random.fold_in(rng, 2), number_of)]


def scatter_about(rng, shape, deviation, bound, shards=(), kind=jnp.bfloat16):
    array = jax.random.normal(rng, shape, jnp.float32) * deviation
    if len(shards) > 0:
        array = steps_of(rng, shape, shards, -0.22, 0.18) * array
    return jnp.clip(array, min=-bound, max=bound).astype(kind)


def gaussian_with(stream_key, extent, scale, bound, pieces, heavy, kind=jnp.bfloat16):
    entries = scale * jax.random.normal(stream_key, extent, jnp.float32)
    if pieces:
        entries = entries * steps_of(stream_key, extent, pieces, -0.22, 0.18)
    return jnp.clip(with_spikes(entries, jax.random.fold_in(stream_key, 3), *heavy), -bound, bound).astype(kind)


def setup_inputs(seed: int = 0) -> dict:
    arg_keys = jax.random.split(jax.random.key(seed), 6)
    values = scatter_about(arg_keys[0], (STREAMS, SEQ, CH), 1.0, 6.0, ((0, 8), (1, 96)))
    cotangent = gaussian_with(arg_keys[1], (STREAMS, SEQ, CH), 1.0, 6.0, ((0, 8), (1, 96)), (0, 2, 8, 2.0))
    seg_ids = jax.vmap(lambda own: jnp.searchsorted(jnp.cumsum(uneven(own, 4, SEQ, SEQ // 2, 2)), jnp.arange(SEQ), side="right"))(jax.random.split(arg_keys[2], STREAMS)).reshape((STREAMS, SEQ)).astype(jnp.int32)
    filters = scatter_about(arg_keys[3], (GROUPS, TAPS), TAPS ** -0.5, 0.5, ((0, 8),))
    skip_gain = scatter_about(arg_keys[4], (CH,), 0.7, 4.0, ((0, 8),))
    return {"values": values, "cotangent": cotangent, "seg_ids": seg_ids, "filters": filters, "skip_gain": skip_gain}


def toeplitz(pattern, rows, width):
    count = pattern.shape[0]
    tiled = jnp.broadcast_to(pattern[:, None, :], (count, rows, width + 1)).reshape(count, rows * (width + 1))
    return tiled[:, :rows * width].reshape(count, rows, width)

def diagonals(matrix, taps):
    count, rows, width = matrix.shape
    flat = jnp.concatenate([matrix.reshape(count, rows * width), jnp.zeros((count, rows), matrix.dtype)], axis=1)
    bands = flat.reshape(count, rows, width + 1)[:, :, 1:taps + 1]
    return lax.optimization_barrier(jnp.sum(bands, axis=1))[:, ::-1]

def reference(values, cotangent, seg_ids, filters, skip_gain):
    width = TAPS + TOK_DEV
    filt = filters.astype(jnp.float32)
    skip = skip_gain.astype(jnp.float32)
    lead = jnp.concatenate([jnp.zeros((GROUPS, 1), jnp.float32), filt[:, ::-1], jnp.zeros((GROUPS, width - TAPS), jnp.float32)], axis=1)
    trail = jnp.concatenate([filt, jnp.zeros((GROUPS, width + 1 - TAPS), jnp.float32)], axis=1)
    forward = toeplitz(lead, TOK_DEV, width)
    backward = toeplitz(trail, TOK_DEV, width)
    zero_rows = jnp.zeros((STREAMS, TAPS, CH), values.dtype)
    vals_pad = jnp.concatenate([zero_rows, values], axis=1)
    cot_pad = jnp.concatenate([cotangent, zero_rows], axis=1)
    filler = jnp.full((STREAMS, TAPS), -1, jnp.int32)
    ids_front = jnp.concatenate([filler, seg_ids.astype(jnp.int32)], axis=1)
    ids_back = jnp.concatenate([seg_ids.astype(jnp.int32), filler], axis=1)
    blocks = SEQ // TOK_DEV
    zero_i = jnp.zeros((), jnp.int32)

    def one(carry, index):
        fgrad, sgrad = carry
        stream = (index // blocks).astype(jnp.int32)
        start = (index % blocks * TOK_DEV).astype(jnp.int32)
        vals_ext = lax.dynamic_slice(vals_pad, (stream, start, zero_i), (1, width, CH))[0].astype(jnp.float32)
        cot_ext = lax.dynamic_slice(cot_pad, (stream, start, zero_i), (1, width, CH))[0].astype(jnp.float32)
        own_vals = vals_ext[TAPS:]
        own_cot = cot_ext[:TOK_DEV]
        own_ids = lax.dynamic_slice(seg_ids.astype(jnp.int32), (stream, start), (1, TOK_DEV))[0]
        prev_ids = lax.dynamic_slice(ids_front, (stream, start), (1, width))[0]
        next_ids = lax.dynamic_slice(ids_back, (stream, start), (1, width))[0]
        mask_prev = (own_ids[:, None] == prev_ids[None, :]).astype(jnp.float32)
        mask_next = (own_ids[:, None] == next_ids[None, :]).astype(jnp.float32)
        vals_g = vals_ext.reshape(width, GROUPS, GSIZE)
        cot_g = cot_ext.reshape(width, GROUPS, GSIZE)
        conv = jnp.einsum('gts,sgc->tgc', forward * mask_prev[None], vals_g).reshape(TOK_DEV, CH)
        mixed = (conv + skip[None, :] * own_vals).astype(jnp.bfloat16)
        adjoint = jnp.einsum('gtr,rgc->tgc', backward * mask_next[None], cot_g).reshape(TOK_DEV, CH)
        grad_vals = (adjoint + skip[None, :] * own_cot).astype(jnp.bfloat16)
        prod = jnp.einsum('tgc,sgc->gts', own_cot.reshape(TOK_DEV, GROUPS, GSIZE), vals_g) * mask_prev[None]
        fgrad = fgrad + diagonals(prod, TAPS)
        sgrad = sgrad + lax.optimization_barrier(jnp.sum(own_cot * own_vals, axis=0))
        return ((fgrad, sgrad), (mixed, grad_vals))
    init = (jnp.zeros((GROUPS, TAPS), jnp.float32), jnp.zeros((CH,), jnp.float32))
    (fgrad, sgrad), (mixed, grad_vals) = lax.scan(one, init, jnp.arange(STREAMS * blocks, dtype=jnp.int32))
    mixed = mixed.reshape(STREAMS, SEQ, CH)
    grad_vals = grad_vals.reshape(STREAMS, SEQ, CH)
    fgrad = fgrad / jnp.sqrt(jnp.float32(STREAMS * SEQ * GSIZE))
    sgrad = sgrad / jnp.sqrt(jnp.float32(STREAMS * SEQ))
    return (mixed, grad_vals, fgrad, sgrad)
```

```python
import functools

import jax
import jax.numpy as jnp
from jax import lax
from jax.experimental import pallas as pl
from jax.experimental.pallas import tpu as pltpu
from jax.sharding import PartitionSpec as P

MESH = pl.DeviceIdType.MESH
LANES = 128
BLOCK = 256
F32 = jnp.float32
BF16 = jnp.bfloat16


def divide(extent, unit):
    return (extent + unit - 1) // unit


def kernel(
    sizes,
    values, cotangent, ids, filt, skip,
    mixed, gvals, fgrad, sgrad,
    v1, c1, v0, c2, mix_buf, adj_buf, ids_prev, ids_next, filt_all, skip_all,
    taps_buf, base_f, base_a, mask_f, mask_a, mask_g, lhs_f, lhs_a, lhs_g, row_acc,
    part, part_in, y_in, z_in, z_own, y_own, final,
    load_sem, store_sem, halo_send, halo_recv, ids_send, ids_recv, filt_send, filt_recv,
    skip_send, skip_recv, part_send, part_recv, y_send, y_recv, z_send, z_recv, g_send, g_recv,
):
    ring, fs, ny, f_scale, s_scale = sizes
    nz = ring // ny
    rows = v1.shape[0]
    width = v1.shape[1] // fs
    groups = filt.shape[0]
    gsize = width // groups
    per_block = BLOCK // gsize
    blocks = width // BLOCK
    piece = part.shape[1] // ny
    grows = groups // ny
    srow_all = width // LANES
    ctx = lax.axis_index("ctx")
    me = lax.axis_index("fsdp")
    zz, yy = ctx // ny, lax.rem(ctx, ny)
    ahead, behind = lax.rem(ctx + 1, ring), lax.rem(ctx + ring - 1, ring)

    def chunk_of(k):
        return lax.rem(me + 1 + k, fs)

    def columns(k):
        return pl.ds(pl.multiple_of(chunk_of(k) * width, width), width)

    loads = [
        pltpu.make_async_copy(values.at[0], v1, load_sem.at[0]),
        pltpu.make_async_copy(cotangent.at[0], c1, load_sem.at[1]),
    ]
    for load in loads:
        load.start()

    barrier = pltpu.get_barrier_semaphore()
    peers = [(ahead, me), (behind, me)]
    peers += [(ctx, lax.rem(me + d, fs)) for d in range(1, fs)]
    peers += [(zz * ny + lax.rem(yy + d, ny), me) for d in range(1, ny)]
    peers += [(lax.rem(zz + d, nz) * ny + yy, me) for d in range(1, nz)]
    for peer in peers:
        pl.semaphore_signal(barrier, inc=1, device_id=peer, device_id_type=MESH)
    pl.semaphore_wait(barrier, len(peers))

    def remote(src, dst, send, recv, peer):
        return pltpu.make_async_remote_copy(
            src_ref=src, dst_ref=dst, send_sem=send, recv_sem=recv,
            device_id=peer, device_id_type=MESH,
        )

    def filt_copy(d):
        return remote(filt, filt_all.at[me], filt_send.at[d - 1], filt_recv.at[d - 1],
                      (ctx, lax.rem(me + d, fs)))

    def skip_copy(d):
        return remote(skip, skip_all.at[me], skip_send.at[d - 1], skip_recv.at[d - 1],
                      (ctx, lax.rem(me + d, fs)))

    def vals_copy(k):
        return remote(values.at[0, :, columns(k)], v0.at[:, columns(k)],
                      halo_send.at[0, k], halo_recv.at[0, k], (ahead, me))

    def cots_copy(k):
        return remote(cotangent.at[0, :, columns(k)], c2.at[:, columns(k)],
                      halo_send.at[1, k], halo_recv.at[1, k], (behind, me))

    def part_copy(k):
        return remote(part.at[k], part_in.at[k], part_send.at[k], part_recv.at[k],
                      (ctx, chunk_of(k)))

    ids_copies = [
        remote(ids, ids_prev, ids_send.at[0], ids_recv.at[0], (ahead, me)),
        remote(ids, ids_next, ids_send.at[1], ids_recv.at[1], (behind, me)),
    ]
    for copy in ids_copies:
        copy.start()
    for d in range(fs - 1, 0, -1):
        filt_copy(d).start()
        skip_copy(d).start()

    def send_halo(k, carry):
        vals_copy(k).start()
        cots_copy(k).start()
        return carry

    lax.fori_loop(0, fs, send_halo, 0)

    filt_all[me] = filt[...]
    skip_all[me] = skip[...]
    row = lax.broadcasted_iota(jnp.int32, (rows, rows), 0)
    lane = lax.broadcasted_iota(jnp.int32, (rows, rows), 1)
    perm = jnp.where(lax.rem(row + lane, rows) == 0, 1.0, 0.0).astype(BF16)
    for copy in ids_copies:
        copy.wait()
    own = jnp.broadcast_to(ids[...].astype(F32), (rows, rows))
    own_col = own.T
    edge_prev = jnp.where(ctx == 0, -1.0, 0.0)
    edge_next = jnp.where(ctx == ring - 1, -1.0, 0.0)
    prev = jnp.broadcast_to(ids_prev[...].astype(F32), (rows, rows))
    prev = jnp.where(edge_prev < 0, -1.0, prev)
    after = jnp.broadcast_to(ids_next[...].astype(F32), (rows, rows))
    after = jnp.where(edge_next < 0, -1.0, after)
    same = own_col == own
    mask_f[:, :rows] = jnp.where(same & (lane <= row), 1.0, 0.0).astype(BF16)
    mask_f[:, rows:] = jnp.where((own_col == prev) & (lane > row), 1.0, 0.0).astype(BF16)
    m1 = jnp.where(same & (lane >= row), 1.0, 0.0)
    m2 = jnp.where((own_col == after) & (lane < row), 1.0, 0.0)
    mask_a[:, :rows] = m1.astype(BF16)
    mask_a[:, rows:] = m2.astype(BF16)
    mask_g[...] = m1 + m2
    upper = lane >= row
    group_lane = lax.broadcasted_iota(jnp.int32, (rows, BLOCK), 1) // gsize
    sub = 16
    steps = rows // sub
    for load in loads:
        load.wait()

    def store_copies(k):
        return (
            pltpu.make_async_copy(
                mix_buf.at[:, columns(k)], mixed.at[0, :, columns(k)], store_sem.at[0, k]),
            pltpu.make_async_copy(
                adj_buf.at[:, columns(k)], gvals.at[0, :, columns(k)], store_sem.at[1, k]),
        )

    def one_chunk(k, carry):
        chunk = chunk_of(k)

        @pl.when(k < fs - 1)
        def _():
            filt_copy(fs - 1 - k).wait_recv()
            skip_copy(fs - 1 - k).wait_recv()

        taps = filt_all[chunk]
        taps_buf[:groups] = jnp.dot(taps, perm, preferred_element_type=F32)
        taps_buf[groups:] = taps.astype(F32)

        def spread(g, inner):
            at = pl.ds(pl.multiple_of(g * sub, sub), sub)
            wide = jnp.broadcast_to(taps_buf[pl.ds(g, 1), :], (sub, rows))
            base_f[at, :] = pltpu.roll(wide, 0, 1, stride=1, stride_axis=0).astype(BF16)
            wide = jnp.broadcast_to(taps_buf[pl.ds(groups + g, 1), :], (sub, rows))
            base_a[at, :] = pltpu.roll(wide, 0, 1, stride=1, stride_axis=0).astype(BF16)
            return inner

        lax.fori_loop(0, groups, spread, 0, unroll=8)
        vals_copy(k).wait_recv()
        cots_copy(k).wait_recv()
        gains = skip_all[chunk].astype(F32)
        for b in range(blocks):
            cs = pl.ds(pl.multiple_of(chunk * width + b * BLOCK, BLOCK), BLOCK)
            vb, cb = v1[:, cs], c1[:, cs]
            wf = jnp.concatenate([vb, v0[:, cs]], axis=0)
            wa = jnp.concatenate([cb, c2[:, cs]], axis=0)
            at = slice(b * per_block * sub, (b + 1) * per_block * sub)
            bf, ba = base_f[at, :], base_a[at, :]
            for s in range(steps):
                here = slice(s * sub, (s + 1) * sub)
                x = (bf if s == 0 else pltpu.roll(bf, s * sub, 1)).reshape(per_block, sub, rows)
                lhs_f[:, here, :rows] = x * mask_f[here, :rows][None]
                lhs_f[:, here, rows:] = x * mask_f[here, rows:][None]
                x = (ba if s == 0 else pltpu.roll(ba, s * sub, 1)).reshape(per_block, sub, rows)
                lhs_a[:, here, :rows] = x * mask_a[here, :rows][None]
                lhs_a[:, here, rows:] = x * mask_a[here, rows:][None]
            for i in range(per_block):
                lhs_g[i] = jnp.where(group_lane == i, vb, jnp.zeros_like(vb))
            flat = (per_block * rows, BLOCK)
            cube = (per_block, rows, BLOCK)
            rf = jnp.dot(lhs_f[...].reshape(flat), wf, preferred_element_type=F32).reshape(cube)
            ra = jnp.dot(lhs_a[...].reshape(flat), wa, preferred_element_type=F32).reshape(cube)
            rg = lax.dot_general(
                lhs_g[...].reshape(flat), wa, (((1,), (1,)), ((), ())), preferred_element_type=F32
            ).reshape(cube)
            vf, cf = vb.astype(F32), cb.astype(F32)
            sums = jnp.sum(vf * cf, axis=0, keepdims=True)
            half = LANES // gsize
            for h in range(BLOCK // LANES):
                ls = slice(h * LANES, (h + 1) * LANES)
                q = b * (BLOCK // LANES) + h
                to = pl.ds(pl.multiple_of(chunk * width + q * LANES, LANES), LANES)
                for result, out, x in ((rf, mix_buf, vf), (ra, adj_buf, cf)):
                    acc = result[h * half, :, ls]
                    for i in range(1, half):
                        acc = jnp.where(group_lane[:, ls] == h * half + i,
                                        result[h * half + i, :, ls], acc)
                    acc = acc + gains[q:q + 1, :] * x[:, ls]
                    out[:, to] = acc.astype(BF16)
                part[k, pl.ds((q % ny) * piece + grows + q // ny, 1), :] = sums[:, ls]
            prod = jnp.where(upper[None], rg[:, :, :rows], rg[:, :, rows:]) * mask_g[...][None]
            acc = prod[:, :8, :].reshape(per_block * 8, rows)
            for s in range(1, rows // 8):
                acc = acc + pltpu.roll(
                    prod[:, 8 * s:8 * s + 8, :].reshape(per_block * 8, rows), rows - 8 * s, 1)
            row_acc[b * per_block * 8:(b + 1) * per_block * 8, :] = acc
        for store in store_copies(k):
            store.start()
        total = row_acc[pl.ds(0, groups, stride=8), :]
        for r in range(1, 8):
            total = total + pltpu.roll(row_acc[pl.ds(r, groups, stride=8), :], rows - r, 1)
        for r in range(grows):
            part[k, pl.ds(r, ny, stride=piece), :] = total[r * ny:(r + 1) * ny]

        @pl.when(k < fs - 1)
        def _():
            part_copy(k).start()

        return carry

    part[...] = jnp.zeros_like(part)
    lax.fori_loop(0, fs, one_chunk, 0)

    total = part[fs - 1]
    for k in range(fs - 1):
        part_copy(k).wait_recv()
        total = total + part_in[k]
    y_own[...] = total

    def y_piece(at):
        return pl.ds(pl.multiple_of(at * piece, piece), piece)

    def y_copy(d):
        to = lax.rem(yy + d, ny)
        return remote(y_own.at[y_piece(to), :], y_in.at[d - 1], y_send.at[d - 1], y_recv.at[d - 1],
                      (zz * ny + to, me))

    def z_copy(d):
        return remote(z_own, z_in.at[zz], z_send.at[d - 1], z_recv.at[d - 1],
                      (lax.rem(zz + d, nz) * ny + yy, me))

    def g_copy(d):
        return remote(final.at[yy], final.at[yy], g_send.at[d - 1], g_recv.at[d - 1],
                      (zz * ny + lax.rem(yy + d, ny), me))

    for d in range(1, ny):
        y_copy(d).start()
    mine = y_own[y_piece(yy), :]
    for d in range(1, ny):
        y_copy(d).wait_recv()
        mine = mine + y_in[d - 1]
    z_own[...] = mine
    for d in range(1, nz):
        z_copy(d).start()
    z_in[zz] = mine
    for d in range(1, nz):
        z_copy(d).wait_recv()
    mine = z_in[0]
    for i in range(1, nz):
        mine = mine + z_in[i]
    piece_row = lax.broadcasted_iota(jnp.int32, mine.shape, 0)
    final[yy] = mine * jnp.where(piece_row < grows, f_scale, s_scale)
    for d in range(1, ny):
        g_copy(d).start()
    for d in range(1, ny):
        g_copy(d).wait_recv()
    for p in range(ny):
        block = final[p]
        fgrad[pl.ds(p, grows, stride=ny), :] = block[:grows]
        for q in range(p, srow_all, ny):
            sgrad[q:q + 1, :] = block[grows + q // ny:grows + q // ny + 1]

    for d in range(1, fs):
        filt_copy(d).wait_send()
        skip_copy(d).wait_send()

    def finish(k, carry):
        vals_copy(k).wait_send()
        cots_copy(k).wait_send()
        for store in store_copies(k):
            store.wait()
        return carry

    lax.fori_loop(0, fs, finish, 0)
    for k in range(fs - 1):
        part_copy(k).wait_send()
    for d in range(1, ny):
        y_copy(d).wait_send()
        g_copy(d).wait_send()
    for d in range(1, nz):
        z_copy(d).wait_send()


def shards(ny, values, cotangent, seg_ids, filters, skip_gain):
    ring, fs = lax.axis_size("ctx"), lax.axis_size("fsdp")
    _, rows, channels = values.shape
    groups = filters.shape[0]
    width = channels // fs
    gsize = width // groups
    lines = width // LANES
    nz = ring // ny
    piece = divide(groups // ny + divide(lines, ny), 8) * 8
    per_block = BLOCK // gsize
    f_scale = 1.0 / float(fs * rows * ring * gsize) ** 0.5
    s_scale = 1.0 / float(fs * rows * ring) ** 0.5
    sizes = (ring, fs, ny, f_scale, s_scale)
    vmem = pltpu.VMEM
    dma = pltpu.SemaphoreType.DMA
    block = vmem((rows, channels), BF16)
    lhs = vmem((per_block, rows, BLOCK), BF16)
    outs = pl.pallas_call(
        functools.partial(kernel, sizes),
        out_shape=(
            jax.ShapeDtypeStruct(values.shape, BF16),
            jax.ShapeDtypeStruct(values.shape, BF16),
            jax.ShapeDtypeStruct((groups, rows), F32),
            jax.ShapeDtypeStruct((lines, LANES), F32),
        ),
        in_specs=[pl.BlockSpec(memory_space=pl.ANY)] * 2
        + [pl.BlockSpec(memory_space=pltpu.VMEM)] * 3,
        out_specs=[pl.BlockSpec(memory_space=pl.ANY)] * 2
        + [pl.BlockSpec(memory_space=pltpu.VMEM)] * 2,
        scratch_shapes=[
            block, block, block, block, block, block,
            vmem((1, rows), jnp.int32), vmem((1, rows), jnp.int32),
            vmem((fs, groups, rows), BF16), vmem((fs, lines, LANES), BF16),
            vmem((2 * groups, rows), F32),
            vmem((groups * 16, rows), BF16), vmem((groups * 16, rows), BF16),
            vmem((rows, BLOCK), BF16), vmem((rows, BLOCK), BF16), vmem((rows, rows), F32),
            lhs, lhs, lhs,
            vmem((groups * 8, rows), F32),
            vmem((fs, ny * piece, LANES), F32), vmem((fs, ny * piece, LANES), F32),
            vmem((ny, piece, LANES), F32), vmem((nz, piece, LANES), F32),
            vmem((piece, LANES), F32), vmem((ny * piece, LANES), F32),
            vmem((ny, piece, LANES), F32),
            dma((2,)), dma((2, fs)), dma((2, fs)), dma((2, fs)), dma((2,)), dma((2,)),
            dma((fs,)), dma((fs,)), dma((fs,)), dma((fs,)), dma((fs,)), dma((fs,)),
            dma((ny,)), dma((ny,)), dma((nz,)), dma((nz,)), dma((ny,)), dma((ny,)),
        ],
        compiler_params=pltpu.CompilerParams(
            collective_id=0, has_side_effects=True, vmem_limit_bytes=56 << 20
        ),
    )(values, cotangent, seg_ids, filters, skip_gain.reshape(lines, LANES))
    mixed, gvals, fgrad, sgrad = outs
    return mixed, gvals, fgrad, sgrad.reshape(width)


def solution(mesh, ny=8):
    placed = (
        P("fsdp", "ctx", None),
        P("fsdp", "ctx", None),
        P("fsdp", "ctx"),
        P("fsdp", None),
        P("fsdp"),
    )
    return jax.shard_map(
        functools.partial(shards, ny),
        mesh=mesh,
        in_specs=placed,
        out_specs=(P("fsdp", "ctx", None), P("fsdp", "ctx", None), P("fsdp", None), P("fsdp")),
        check_vma=False,
    )
```
